32 devices in a mesh: mp: 4 (over y, core), codec: 8 (over z, x).
Axes of the slice: x: 2, y: 2, z: 4, core: 2. Of those that a mesh axis runs over, the one named last changes fastest.
Arguments:
- frames: bfloat16 [4096, 4, 1024], P(('mp', 'codec')), may hold values from -6 to 6
- row_dialogue: int32 [4096], P(('mp', 'codec')), may hold values from 0 to 4095, as said below
- intersection_cache: bfloat16 [4096, 8, 512], P(('mp', 'codec')), may hold values from -6 to 6
- history_cache: bfloat16 [4096, 2, 512], P(('mp', 'codec')), may hold values from -6 to 6
- new_slot: int32 [4096], P(('mp', 'codec')), may hold values from 0 to 4095, as said below
- up_weight: bfloat16 [1024, 8192], replicated, may hold values from -0.1875 to 0.1875
- up_bias: bfloat16 [512], replicated, may hold values from -3 to 3
- dilated_weight: bfloat16 [1536, 256], replicated, may hold values from -0.15625 to 0.15625
- dilated_bias: bfloat16 [256], replicated, may hold values from -3 to 3
- project_weight: bfloat16 [256, 512], replicated, may hold values from -0.375 to 0.375
- project_bias: bfloat16 [512], replicated, may hold values from -3 to 3
Outputs:
- upsampled: bfloat16 [4096, 32, 512], P(('mp', 'codec'))
- next_intersection: bfloat16 [4096, 8, 512], P(('mp', 'codec'))
- next_history: bfloat16 [4096, 2, 512], P(('mp', 'codec'))
The draws below stay inside these ranges and needn't reach their ends.
Inputs may be any that keep to these rules, and one draw needn't show every extreme that they name: `row_dialogue`: A permutation of the 4096 dialogues; dialogue g is held by device g // 128. The 128 rows of one device name at most 8 dialogues held by any one device, and exactly 8 of some device. `new_slot`: A permutation of the 4096 slots; slot h lies on device h // 128. The 128 dialogues of one device move to at most 8 slots of any one device, and exactly 8 of some device.
All inputs are finite; a program needn't handle non-finite values.
Results may differ from the reference program's by a relative error of at most 0.0052.
Values may be sent and summed in bfloat16 or wider, within the bound.
No kernel may reach another device: no remote copies, remote signals or barrier semaphores. Data moves between devices by JAX's collectives and lax.ppermute only.
A program may use at most 192 MiB of HBM per device.

```python
import jax
import jax.numpy as jnp
from jax import lax

C = 1024
H = 512
R = 256
FR = 4
STRIDE = 8
KR = 3
DLG = 128
CAP = 8
G = 4096


def permuted_slots(key):
    device_count = G // DLG
    keys = jax.random.split(key, 4)
    pool = jax.random.permutation(keys[0], device_count * CAP)
    first_block = pool[0] // CAP
    outside = (pool // CAP == first_block).astype(jnp.int32)
    remaining = pool[jnp.argsort(outside, stable=True)]
    entries = jnp.concatenate([first_block * CAP + jnp.arange(CAP, dtype=jnp.int32), remaining[:DLG - CAP].astype(jnp.int32)])
    offsets = entries // CAP
    order_keys = jax.random.randint(keys[1], (device_count, DLG), 0, 1 << 20) * DLG + jnp.arange(DLG, dtype=jnp.int32)[None, :]
    row_order = jnp.argsort(order_keys, axis=1)
    row_offsets = offsets[row_order]
    relabel = jax.random.permutation(keys[2], device_count).astype(jnp.int32)
    inverse = jnp.argsort(relabel).astype(jnp.int32)
    sources = jnp.arange(device_count, dtype=jnp.int32)[:, None]
    destination = relabel[(inverse[sources] + row_offsets) % device_count]
    tiebreak = jax.random.permutation(keys[3], G).astype(jnp.int32)
    sort_key = destination.reshape(-1) * G + tiebreak
    sorted_order = jnp.argsort(sort_key)
    return jnp.zeros((G,), jnp.int32).at[sorted_order].set(jnp.arange(G, dtype=jnp.int32))


def draw_row_dialogue(key, part):
    return permuted_slots(jax.random.fold_in(key, 11))


def draw_new_slot(key, part):
    return permuted_slots(jax.random.fold_in(key, 23))


def block_scale(key, extent, cuts, least, largest):
    level = 1.0
    for position, blocks in cuts:
        heights = jax.random.uniform(jax.random.fold_in(jax.random.fold_in(key, 6), position), (blocks,), jnp.float32, least / len(cuts), largest / len(cuts))
        level = level * jnp.repeat(jnp.exp(heights), extent[position] // blocks).reshape((-1,) + (1,) * (len(extent) - 1 - position))
    return level


def scatter_about(rng, shape, spread, bound, cuts=(), held_as=jnp.bfloat16):
    drawn = jax.random.normal(rng, shape, jnp.float32) * spread
    if len(cuts) > 0:
        drawn = block_scale(rng, shape, cuts, -0.22, 0.18) * drawn
    return jnp.clip(drawn, min=-bound, max=bound).astype(held_as)


def setup_inputs(seed: int = 0) -> dict:
    key_of = jax.random.split(jax.random.key(seed), 12)
    return {
        "frames": scatter_about(key_of[0], (G, FR, C), 1.0, 6.0, ((0, 32),)),
        "row_dialogue": draw_row_dialogue(jax.random.fold_in(key_of[11], 71), 0),
        "intersection_cache": scatter_about(key_of[2], (G, STRIDE, H), 1.0, 6.0, ((0, 32),)),
        "history_cache": scatter_about(key_of[3], (G, KR - 1, H), 1.0, 6.0, ((0, 32),)),
        "new_slot": draw_new_slot(jax.random.fold_in(key_of[11], 71), 0),
        "up_weight": scatter_about(key_of[5], (C, 2 * STRIDE * H), C ** -0.5, 0.1875),
        "up_bias": scatter_about(key_of[6], (H,), 0.5, 3.0),
        "dilated_weight": scatter_about(key_of[7], (KR * H, R), (KR * H) ** -0.5, 0.15625),
        "dilated_bias": scatter_about(key_of[8], (R,), 0.5, 3.0),
        "project_weight": scatter_about(key_of[9], (R, H), R ** -0.5, 0.375),
        "project_bias": scatter_about(key_of[10], (H,), 0.5, 3.0),
    }


def unfold(extended, tap_count, length):
    return jnp.concatenate([extended[:, k:k + length] for k in range(tap_count)], axis=-1)


def decode_block(latent, intersection_cache, history_cache, up_weight, up_bias, dilated_weight, dilated_bias, project_weight, project_bias):
    batch_size, frame_count, channels = latent.shape
    stride = intersection_cache.shape[1]
    hidden = intersection_cache.shape[2]
    active = jax.nn.elu(latent.astype(jnp.float32)).astype(jnp.bfloat16).reshape(batch_size * frame_count, channels)
    halves = jnp.dot(active, up_weight, preferred_element_type=jnp.float32).reshape(batch_size, frame_count, 2, stride, hidden)
    first_half = halves[:, :, 0]
    second = halves[:, :, 1]
    carried = jnp.concatenate([intersection_cache.astype(jnp.float32)[:, None], second[:, :-1]], axis=1)
    length = frame_count * stride
    section_out = (first_half + carried + up_bias.astype(jnp.float32)).astype(jnp.bfloat16).reshape(batch_size, length, hidden)
    section_out = lax.optimization_barrier(section_out)
    joined = jnp.concatenate([history_cache, section_out], axis=1)
    lifted = jax.nn.elu(joined.astype(jnp.float32)).astype(jnp.bfloat16)
    columns_two = unfold(lifted, KR, length).reshape(batch_size * length, KR * hidden)
    inner_pre = jnp.dot(columns_two, dilated_weight, preferred_element_type=jnp.float32) + dilated_bias.astype(jnp.float32)
    inner_act = jax.nn.elu(inner_pre).astype(jnp.bfloat16)
    branch = jnp.dot(inner_act, project_weight, preferred_element_type=jnp.float32) + project_bias.astype(jnp.float32)
    result = (section_out.astype(jnp.float32) + branch.reshape(batch_size, length, hidden)).astype(jnp.bfloat16)
    last_active = active.reshape(batch_size, frame_count, channels)[:, -1]
    intersection_next = second[:, -1].astype(jnp.bfloat16)
    return result, last_active, intersection_next, section_out[:, length - (KR - 1):]


def reference(frames, row_dialogue, intersection_cache, history_cache, new_slot, up_weight, up_bias, dilated_weight, dilated_bias, project_weight, project_bias):
    dialogues = frames.shape[0]
    block_count = dialogues // DLG
    ordered = jnp.zeros_like(frames).at[row_dialogue].set(frames)

    def shaped(array):
        return array.reshape((block_count, DLG) + array.shape[1:])

    def decode_one(blocks):
        latent, intersections, histories = blocks
        return decode_block(latent, intersections, histories, up_weight, up_bias, dilated_weight, dilated_bias, project_weight, project_bias)

    decoded = lax.map(decode_one, (shaped(ordered), shaped(intersection_cache), shaped(history_cache)))
    flattened = [output_part.reshape((dialogues,) + output_part.shape[2:]) for output_part in decoded]
    upsampled = flattened[0]
    next_intersection = jnp.zeros_like(flattened[2]).at[new_slot].set(flattened[2])
    next_history = jnp.zeros_like(flattened[3]).at[new_slot].set(flattened[3])
    return (upsampled, next_intersection, next_history)
```

```python
import jax
import jax.numpy as jnp
from jax import lax
from jax.experimental import pallas as pl
from jax.experimental.pallas import tpu as pltpu
from jax.sharding import PartitionSpec as P

AXES = ("mp", "codec")
BF16 = jnp.bfloat16
F32 = jnp.float32
I32 = jnp.int32
LANES = 128


def elu(v):
    return jnp.maximum(v, jnp.exp(jnp.minimum(v, 0.0)) - 1.0)


def split_index(index, local_count):
    if local_count & (local_count - 1) == 0:
        shift = local_count.bit_length() - 1
        return index >> shift, index & (local_count - 1)
    return lax.div(index, local_count), lax.rem(index, local_count)


def column_of(row):
    n = row.shape[1]
    eye = lax.broadcasted_iota(I32, (n, n), 0) == lax.broadcasted_iota(I32, (n, n), 1)
    return jnp.sum(jnp.where(eye, jnp.broadcast_to(row, (n, n)), 0), axis=1, keepdims=True)


def row_of(column):
    n = column.shape[0]
    eye = lax.broadcasted_iota(I32, (n, n), 0) == lax.broadcasted_iota(I32, (n, n), 1)
    return jnp.sum(jnp.where(eye, jnp.broadcast_to(column, (n, n)), 0), axis=0, keepdims=True)


def bucket_selector(target_row, local_count, capacity, rows):
    n = target_row.shape[1]
    owner, within = split_index(target_row, local_count)
    owner_column = column_of(owner)
    earlier = lax.broadcasted_iota(I32, (n, n), 0) < lax.broadcasted_iota(I32, (n, n), 1)
    same = (owner_column == owner) & earlier
    rank = jnp.sum(same.astype(I32), axis=0, keepdims=True)
    position = owner * capacity + rank
    chosen = lax.broadcasted_iota(I32, (rows, n), 0) == position
    slots = local_count + jnp.sum(jnp.where(chosen, within - local_count, 0), axis=1, keepdims=True)
    return chosen.astype(F32).astype(BF16), slots


def settle_selector(slots_column, local_count):
    rows = slots_column.shape[0]
    slots = row_of(slots_column)
    chosen = lax.broadcasted_iota(I32, (local_count, rows), 0) == slots
    return chosen.astype(F32).astype(BF16)


def pick(selector, rows):
    return jnp.dot(selector, rows, preferred_element_type=F32).astype(BF16)


def bucket_kernel(target_ref, frames_ref, out_ref, *, local_count, capacity):
    frame_count, channels = frames_ref.shape[1:]
    rows = out_ref.shape[0]
    selector, slots = bucket_selector(target_ref[...], local_count, capacity, rows)
    for t in range(frame_count):
        active = elu(frames_ref[:, t, :].astype(F32)).astype(BF16)
        out_ref[:, t * channels : (t + 1) * channels] = pick(selector, active)
    width = frame_count * channels
    out_ref[:, width:] = jnp.broadcast_to(slots.astype(F32), (rows, LANES)).astype(BF16)


def forward_kernel(arrived_ref, target_ref, active_ref, out_ref, *, local_count, capacity):
    frame_count, _, channels = active_ref.shape
    rows = out_ref.shape[0]
    width = frame_count * channels
    slots = arrived_ref[:, width : width + LANES].astype(F32)[:, :1].astype(I32)
    settle = settle_selector(slots, local_count)
    for t in range(frame_count):
        active_ref[t] = pick(settle, arrived_ref[:, t * channels : (t + 1) * channels])
    selector, out_slots = bucket_selector(target_ref[...], local_count, capacity, rows)
    for n in range(2):
        out_ref[:, n * channels : (n + 1) * channels] = pick(selector, active_ref[frame_count - 2 + n])
    out_ref[:, 2 * channels :] = jnp.broadcast_to(out_slots.astype(F32), (rows, LANES)).astype(BF16)


def decode_kernel(
    active_ref,
    first_ref,
    second_ref,
    carried_ref,
    history_ref,
    up_bias_ref,
    dilated_ref,
    dilated_bias_ref,
    project_ref,
    project_bias_ref,
    out_ref,
    section_ref,
    lifted_ref,
    turned_ref,
    *,
    stride,
    block,
):
    frame_count, local_count, channels = active_ref.shape
    hidden = up_bias_ref.shape[1]
    past = history_ref.shape[0]
    taps = past + 1
    length = frame_count * stride
    step = pl.program_id(0)

    @pl.when(step == 0)
    def _():
        lifted_ref[0:past] = elu(history_ref[...].astype(F32)).astype(BF16)

    @pl.when(step < stride)
    def _():
        active = active_ref[...].reshape(frame_count * local_count, channels)
        first = jnp.dot(active, first_ref[...], preferred_element_type=F32)
        second = jnp.dot(active, second_ref[...], preferred_element_type=F32)
        bias = up_bias_ref[...].astype(F32)
        for t in range(frame_count):
            now = first[t * local_count : (t + 1) * local_count]
            if t == 0:
                before = carried_ref[0].astype(F32)
            else:
                before = second[(t - 1) * local_count : t * local_count]
            section = (now + before + bias).astype(BF16)
            section_ref[t * stride + step] = section
            lifted_ref[past + t * stride + step] = elu(section.astype(F32)).astype(BF16)

    @pl.when(step >= stride)
    def _():
        start = pl.multiple_of((step - stride) * block, block)
        inner = dilated_bias_ref[...].astype(F32)
        for k in range(taps):
            window = lifted_ref[k : k + length, pl.ds(start, block), :].reshape(length * block, hidden)
            inner = inner + jnp.dot(window, dilated_ref[k * hidden : (k + 1) * hidden], preferred_element_type=F32)
        inner = elu(inner).astype(BF16)
        branch = jnp.dot(inner, project_ref[...], preferred_element_type=F32) + project_bias_ref[...].astype(F32)
        section = section_ref[:, pl.ds(start, block), :].reshape(length * block, hidden)
        result = section.astype(F32) + branch
        for c in range(hidden // LANES):
            lanes = slice(c * LANES, (c + 1) * LANES)
            for j in range(length):
                turned_ref[c, pl.ds(j, block, stride=length), :] = result[j * block : (j + 1) * block, lanes]
            out_ref[:, :, lanes] = turned_ref[c].astype(BF16).reshape(block, length, LANES)


def caches_kernel(arrived_ref, early_ref, late_ref, up_bias_ref, inter_ref, hist_ref, active_ref, turned_ref, *, stride, past):
    _, local_count, channels = active_ref.shape
    hidden = up_bias_ref.shape[1]
    step = pl.program_id(0)

    @pl.when(step == 0)
    def _():
        slots = arrived_ref[:, 2 * channels :].astype(F32)[:, :1].astype(I32)
        settle = settle_selector(slots, local_count)
        for n in range(2):
            active_ref[n] = pick(settle, arrived_ref[:, n * channels : (n + 1) * channels])

    second = jnp.dot(active_ref[1], late_ref[...], preferred_element_type=F32)
    for c in range(hidden // LANES):
        turned_ref[c, pl.ds(step, local_count, stride=stride), :] = second[:, c * LANES : (c + 1) * LANES]

    for j in range(past):
        @pl.when(step == stride - past + j)
        def _():
            section = (
                jnp.dot(active_ref[1], early_ref[...], preferred_element_type=F32)
                + jnp.dot(active_ref[0], late_ref[...], preferred_element_type=F32)
                + up_bias_ref[...].astype(F32)
            )
            hist_ref[:, j * hidden : (j + 1) * hidden] = section.astype(BF16)

    @pl.when(step == stride - 1)
    def _():
        for c in range(hidden // LANES):
            inter_ref[:, :, c * LANES : (c + 1) * LANES] = (
                turned_ref[c].reshape(local_count, stride, LANES).astype(BF16)
            )


def exchange(rows, device_count, capacity):
    width = rows.shape[1]
    moved = lax.all_to_all(
        rows.reshape(device_count, capacity, width), AXES, split_axis=0, concat_axis=0, tiled=True
    )
    return moved.reshape(device_count * capacity, width)


def local(
    frames,
    row_dialogue,
    intersection_cache,
    history_cache,
    new_slot,
    up_weight,
    up_bias,
    dilated_weight,
    dilated_bias,
    project_weight,
    project_bias,
):
    local_count, frame_count, channels = frames.shape
    stride, hidden = intersection_cache.shape[1:]
    past = history_cache.shape[1]
    length = frame_count * stride
    residual = dilated_weight.shape[1]
    device_count = lax.axis_size("mp") * lax.axis_size("codec")
    capacity = 2 * local_count // device_count
    rows = device_count * capacity
    block = 16
    big = pltpu.CompilerParams(vmem_limit_bytes=56 * 1024 * 1024)
    up_bias = up_bias[None]
    dilated_bias = dilated_bias[None]
    project_bias = project_bias[None]
    row_dialogue = row_dialogue[None]
    new_slot = new_slot[None]

    outgoing = pl.pallas_call(
        lambda *refs: bucket_kernel(*refs, local_count=local_count, capacity=capacity),
        out_shape=jax.ShapeDtypeStruct((rows, frame_count * channels + LANES), BF16),
        compiler_params=big,
        name="bucket",
    )(row_dialogue, frames)
    arrived = exchange(outgoing, device_count, capacity)

    active, forwarded = pl.pallas_call(
        lambda *refs: forward_kernel(*refs, local_count=local_count, capacity=capacity),
        out_shape=(
            jax.ShapeDtypeStruct((frame_count, local_count, channels), BF16),
            jax.ShapeDtypeStruct((rows, 2 * channels + LANES), BF16),
        ),
        compiler_params=big,
        name="forward",
    )(arrived, new_slot)
    arrived_caches = exchange(forwarded, device_count, capacity)

    carried = jnp.swapaxes(intersection_cache, 0, 1)
    history = jnp.swapaxes(history_cache, 0, 1)
    last = stride - 1

    def whole(shape):
        return pl.BlockSpec(shape, lambda i: (0,) * len(shape))

    upsampled = pl.pallas_call(
        lambda *refs: decode_kernel(*refs, stride=stride, block=block),
        grid=(stride + local_count // block,),
        in_specs=[
            whole((frame_count, local_count, channels)),
            pl.BlockSpec((channels, hidden), lambda i: (0, jnp.minimum(i, last))),
            pl.BlockSpec((channels, hidden), lambda i: (0, stride + jnp.minimum(i, last))),
            pl.BlockSpec((1, local_count, hidden), lambda i: (jnp.minimum(i, last), 0, 0)),
            whole((past, local_count, hidden)),
            whole((1, hidden)),
            whole(dilated_weight.shape),
            whole((1, residual)),
            whole(project_weight.shape),
            whole((1, hidden)),
        ],
        out_specs=pl.BlockSpec((block, length, hidden), lambda i: (jnp.maximum(i - stride, 0), 0, 0)),
        out_shape=jax.ShapeDtypeStruct((local_count, length, hidden), BF16),
        scratch_shapes=[
            pltpu.VMEM((length, local_count, hidden), BF16),
            pltpu.VMEM((past + length, local_count, hidden), BF16),
            pltpu.VMEM((hidden // LANES, block * length, LANES), F32),
        ],
        compiler_params=big,
        name="decode",
    )(
        active,
        up_weight,
        up_weight,
        carried,
        history,
        up_bias,
        dilated_weight,
        dilated_bias,
        project_weight,
        project_bias,
    )

    next_intersection, next_history = pl.pallas_call(
        lambda *refs: caches_kernel(*refs, stride=stride, past=past),
        grid=(stride,),
        in_specs=[
            whole((rows, 2 * channels + LANES)),
            pl.BlockSpec((channels, hidden), lambda i: (0, jnp.maximum(i, stride - past))),
            pl.BlockSpec((channels, hidden), lambda i: (0, stride + i)),
            whole((1, hidden)),
        ],
        out_specs=(
            whole((local_count, stride, hidden)),
            whole((local_count, past * hidden)),
        ),
        out_shape=(
            jax.ShapeDtypeStruct((local_count, stride, hidden), BF16),
            jax.ShapeDtypeStruct((local_count, past * hidden), BF16),
        ),
        scratch_shapes=[
            pltpu.VMEM((2, local_count, channels), BF16),
            pltpu.VMEM((hidden // LANES, local_count * stride, LANES), F32),
        ],
        compiler_params=big,
        name="caches",
    )(arrived_caches, up_weight, up_weight, up_bias)
    return (upsampled, next_intersection, next_history.reshape(local_count, past, hidden))


def solution(mesh):
    split = P(AXES)
    in_specs = (split,) * 5 + (P(),) * 6
    return jax.shard_map(local, mesh=mesh, in_specs=in_specs, out_specs=(split,) * 3, check_vma=False)
```

```python
import jax
import jax.numpy as jnp
from jax import lax
from jax.experimental import pallas as pl
from jax.experimental.pallas import tpu as pltpu
from jax.sharding import PartitionSpec as P

AXES = ("mp", "codec")
BF16 = jnp.bfloat16
F32 = jnp.float32
I32 = jnp.int32
LANES = 128


def elu(v):
    return jnp.maximum(v, jnp.exp(jnp.minimum(v, 0.0)) - 1.0)


def split_index(index, local_count):
    if local_count & (local_count - 1) == 0:
        shift = local_count.bit_length() - 1
        return index >> shift, index & (local_count - 1)
    return lax.div(index, local_count), lax.rem(index, local_count)


def column_of(row):
    n = row.shape[1]
    eye = lax.broadcasted_iota(I32, (n, n), 0) == lax.broadcasted_iota(I32, (n, n), 1)
    return jnp.sum(jnp.where(eye, jnp.broadcast_to(row, (n, n)), 0), axis=1, keepdims=True)


def row_of(column):
    n = column.shape[0]
    eye = lax.broadcasted_iota(I32, (n, n), 0) == lax.broadcasted_iota(I32, (n, n), 1)
    return jnp.sum(jnp.where(eye, jnp.broadcast_to(column, (n, n)), 0), axis=0, keepdims=True)


def bucket_selector(target_row, local_count, capacity, rows):
    n = target_row.shape[1]
    owner, within = split_index(target_row, local_count)
    owner_column = column_of(owner)
    earlier = lax.broadcasted_iota(I32, (n, n), 0) < lax.broadcasted_iota(I32, (n, n), 1)
    same = (owner_column == owner) & earlier
    rank = jnp.sum(same.astype(I32), axis=0, keepdims=True)
    position = owner * capacity + rank
    chosen = lax.broadcasted_iota(I32, (rows, n), 0) == position
    slots = local_count + jnp.sum(jnp.where(chosen, within - local_count, 0), axis=1, keepdims=True)
    return chosen.astype(F32).astype(BF16), slots


def settle_selector(slots_column, local_count):
    rows = slots_column.shape[0]
    slots = row_of(slots_column)
    chosen = lax.broadcasted_iota(I32, (local_count, rows), 0) == slots
    return chosen.astype(F32).astype(BF16)


def pick(selector, rows):
    return jnp.dot(selector, rows, preferred_element_type=F32).astype(BF16)


def slot_lanes(slots, rows):
    return jnp.broadcast_to(slots.astype(F32), (rows, LANES))


def turner(outer, inner):
    n = outer * inner
    target = lax.broadcasted_iota(I32, (n, n), 0)
    origin = lax.broadcasted_iota(I32, (n, n), 1)
    wanted = lax.rem(target, inner) * outer + lax.div(target, inner)
    return (origin == wanted).astype(F32).astype(BF16)


def bucket_kernel(target_ref, later_ref, frames_ref, out_ref, *, local_count, capacity):
    rows = out_ref.shape[0]
    width = frames_ref.shape[1]
    chunk = width // 4
    selector, slots = bucket_selector(target_ref[...], local_count, capacity, rows)
    _, later_slots = bucket_selector(later_ref[...], local_count, capacity, rows)
    lane = lax.broadcasted_iota(I32, (rows, LANES), 1)
    tags = jnp.where(lane == 0, slot_lanes(slots, rows), slot_lanes(later_slots, rows))
    out_ref[:, width:] = tags.astype(BF16)
    for c in range(4):
        lanes = slice(c * chunk, (c + 1) * chunk)
        out_ref[:, lanes] = pick(selector, elu(frames_ref[:, lanes].astype(F32)).astype(BF16))


def forward_kernel(arrived_ref, target_ref, out_ref, tags_ref, *, local_count, capacity):
    rows = out_ref.shape[0]
    width = out_ref.shape[1]
    skip = arrived_ref.shape[1] - LANES - width
    tags = arrived_ref[:, skip + width :]
    tags_ref[...] = tags
    settle = settle_selector(tags.astype(F32)[:, :1].astype(I32), local_count)
    selector, _ = bucket_selector(target_ref[...], local_count, capacity, rows)
    selector = pick(selector, settle)
    half = width // 2
    for n in range(2):
        lanes = slice(skip + n * half, skip + (n + 1) * half)
        out_ref[:, n * half : (n + 1) * half] = pick(selector, arrived_ref[:, lanes])


def decode_kernel(
    arrived_ref,
    weight_ref,
    carried_ref,
    history_ref,
    up_bias_ref,
    dilated_ref,
    dilated_bias_ref,
    project_ref,
    project_bias_ref,
    out_ref,
    active_ref,
    section_ref,
    lifted_ref,
    turn_ref,
    held_ref,
    sems,
    *,
    stride,
    block,
):
    frame_count, local_count, channels = active_ref.shape
    hidden = up_bias_ref.shape[1]
    past = history_ref.shape[0]
    taps = past + 1
    length = frame_count * stride
    step = pl.program_id(0)

    def fetch(tap):
        return pltpu.make_async_copy(weight_ref.at[:, pl.ds(tap * hidden, hidden)], held_ref.at[tap], sems.at[tap])

    @pl.when(step == 0)
    def _():
        for s in range(stride):
            fetch(s).start()
            fetch(stride + s).start()
        lifted_ref[0:past] = elu(history_ref[...].astype(F32)).astype(BF16)
        turn_ref[...] = turner(block, block)
        width = frame_count * channels
        settle = settle_selector(arrived_ref[:, width:].astype(F32)[:, :1].astype(I32), local_count)
        for t in range(frame_count):
            active_ref[t] = pick(settle, arrived_ref[:, t * channels : (t + 1) * channels])

    @pl.when(step < stride)
    def _():
        fetch(step).wait()
        fetch(stride + step).wait()
        active = active_ref[...].reshape(frame_count * local_count, channels)
        first = jnp.dot(active, held_ref[step], preferred_element_type=F32)
        second = jnp.dot(active, held_ref[stride + step], preferred_element_type=F32)
        bias = up_bias_ref[...].astype(F32)
        for t in range(frame_count):
            now = first[t * local_count : (t + 1) * local_count]
            if t == 0:
                before = carried_ref[0].astype(F32)
            else:
                before = second[(t - 1) * local_count : t * local_count]
            section = (now + before + bias).astype(BF16)
            section_ref[t * stride + step] = section
            lifted_ref[past + t * stride + step] = elu(section.astype(F32)).astype(BF16)

    @pl.when(step >= stride)
    def _():
        start = pl.multiple_of((step - stride) * block, block)
        window = jnp.concatenate(
            [
                lifted_ref[k : k + length, pl.ds(start, block), :].reshape(length * block, hidden)
                for k in range(taps)
            ],
            axis=-1,
        )
        inner = jnp.dot(window, dilated_ref[...], preferred_element_type=F32) + dilated_bias_ref[...].astype(F32)
        inner = elu(inner).astype(BF16)
        branch = jnp.dot(inner, project_ref[...], preferred_element_type=F32) + project_bias_ref[...].astype(F32)
        section = section_ref[:, pl.ds(start, block), :].reshape(length * block, hidden)
        result = (section.astype(F32) + branch).astype(BF16)
        for j in range(0, length, block):
            turned = pick(turn_ref[...], result[j * block : (j + block) * block])
            out_ref[:, j : j + block, :] = turned.reshape(block, block, hidden)


def caches_kernel(
    arrived_ref, tags_ref, weight_ref, up_bias_ref, inter_ref, hist_ref, kept_ref, held_ref, sems, *, stride, past
):
    local_count = inter_ref.shape[0]
    channels, hidden = held_ref.shape[1:]

    def fetch(n):
        tap = stride + n if n < stride else n - past
        return pltpu.make_async_copy(weight_ref.at[:, pl.ds(tap * hidden, hidden)], held_ref.at[n], sems.at[n])

    order = [stride - past + j for j in range(past)] + [stride + j for j in range(past)] + list(range(stride - past))
    for n in order:
        fetch(n).start()
    settle = settle_selector(tags_ref[...].astype(F32)[:, 1:2].astype(I32), local_count)
    before, last = [pick(settle, arrived_ref[:, n * channels : (n + 1) * channels]) for n in range(2)]
    sections = []
    for n in order:
        fetch(n).wait()
        if n < stride:
            second = jnp.dot(last, held_ref[n], preferred_element_type=F32)
            kept_ref[n] = second.astype(BF16)
        else:
            section = (
                jnp.dot(last, held_ref[n], preferred_element_type=F32)
                + jnp.dot(before, held_ref[n - past], preferred_element_type=F32)
                + up_bias_ref[...].astype(F32)
            )
            sections.append(section.astype(BF16))
    group = 256 // stride
    turn = turner(group, stride)
    for g in range(0, local_count, group):
        rows = kept_ref[:, g : g + group, :].reshape(stride * group, hidden)
        turned = jnp.dot(turn, rows, preferred_element_type=F32)
        inter_ref[g : g + group] = turned.reshape(group, stride, hidden).astype(BF16)
    turned = jnp.dot(turner(local_count, past), jnp.concatenate(sections, axis=0), preferred_element_type=F32)
    hist_ref[...] = turned.reshape(local_count, past, hidden).astype(BF16)


def exchange(rows, device_count, capacity):
    width = rows.shape[1]
    moved = lax.all_to_all(
        rows.reshape(device_count, capacity, width), AXES, split_axis=0, concat_axis=0, tiled=True
    )
    return moved.reshape(device_count * capacity, width)


BIG = pltpu.CompilerParams(vmem_limit_bytes=40 * 1024 * 1024)
NEAR = pl.BlockSpec(memory_space=pltpu.VMEM)


def near(array):
    return pltpu.with_memory_space_constraint(array, pltpu.VMEM)


def whole(shape):
    return pl.BlockSpec(shape, lambda i: (0,) * len(shape))


def bucket(row_dialogue, new_slot, frames, device_count, capacity):
    local_count, frame_count, channels = frames.shape
    width = frame_count * channels
    return pl.pallas_call(
        lambda *refs: bucket_kernel(*refs, local_count=local_count, capacity=capacity),
        out_shape=pltpu.HBM((device_count * capacity, width + LANES), BF16),
        compiler_params=BIG,
        name="bucket",
    )(row_dialogue, new_slot, frames.reshape(local_count, width))


def forward(arrived, new_slot, width, capacity):
    local_count = new_slot.shape[1]
    rows = arrived.shape[0]
    return pl.pallas_call(
        lambda *refs: forward_kernel(*refs, local_count=local_count, capacity=capacity),
        out_shape=(
            pltpu.HBM((rows, width), BF16),
            pltpu.VMEM((rows, LANES), BF16),
        ),
        compiler_params=BIG,
        name="forward",
    )(near(arrived), new_slot)


def decode(
    arrived, carried, history, up_weight, up_bias, dilated_weight, dilated_bias, project_weight, project_bias,
):
    channels = up_weight.shape[0]
    frame_count = arrived.shape[1] // channels
    stride, local_count, hidden = carried.shape
    past = history.shape[0]
    length = frame_count * stride
    last = stride - 1
    block = 16
    return pl.pallas_call(
        lambda *refs: decode_kernel(*refs, stride=stride, block=block),
        grid=(stride + local_count // block,),
        in_specs=[
            NEAR,
            pl.BlockSpec(memory_space=pl.ANY),
            pl.BlockSpec((1, local_count, hidden), lambda i: (jnp.minimum(i, last), 0, 0)),
            whole(history.shape),
            whole(up_bias.shape),
            whole(dilated_weight.shape),
            whole(dilated_bias.shape),
            whole(project_weight.shape),
            whole(project_bias.shape),
        ],
        out_specs=pl.BlockSpec((block, length, hidden), lambda i: (jnp.maximum(i - stride, 0), 0, 0)),
        out_shape=jax.ShapeDtypeStruct((local_count, length, hidden), BF16),
        scratch_shapes=[
            pltpu.VMEM((frame_count, local_count, channels), BF16),
            pltpu.VMEM((length, local_count, hidden), BF16),
            pltpu.VMEM((past + length, local_count, hidden), BF16),
            pltpu.VMEM((block * block, block * block), BF16),
            pltpu.VMEM((2 * stride, channels, hidden), BF16),
            pltpu.SemaphoreType.DMA((2 * stride,)),
        ],
        compiler_params=BIG,
        name="decode",
    )(
        near(arrived),
        up_weight,
        carried,
        history,
        up_bias,
        dilated_weight,
        dilated_bias,
        project_weight,
        project_bias,
    )


def caches(arrived, tags, up_weight, up_bias, local_count, stride, past):
    channels = up_weight.shape[0]
    hidden = up_bias.shape[1]
    return pl.pallas_call(
        lambda *refs: caches_kernel(*refs, stride=stride, past=past),
        in_specs=[NEAR, NEAR, pl.BlockSpec(memory_space=pl.ANY), NEAR],
        out_shape=(
            jax.ShapeDtypeStruct((local_count, stride, hidden), BF16),
            jax.ShapeDtypeStruct((local_count, past, hidden), BF16),
        ),
        scratch_shapes=[
            pltpu.VMEM((stride, local_count, hidden), BF16),
            pltpu.VMEM((stride + past, channels, hidden), BF16),
            pltpu.SemaphoreType.DMA((stride + past,)),
        ],
        compiler_params=BIG,
        name="caches",
    )(near(arrived), near(tags), up_weight, up_bias)


def local(
    frames,
    row_dialogue,
    intersection_cache,
    history_cache,
    new_slot,
    up_weight,
    up_bias,
    dilated_weight,
    dilated_bias,
    project_weight,
    project_bias,
):
    local_count, frame_count, channels = frames.shape
    stride, hidden = intersection_cache.shape[1:]
    past = history_cache.shape[1]
    device_count = lax.axis_size("mp") * lax.axis_size("codec")
    capacity = 2 * local_count // device_count
    new_slot = new_slot[None]

    outgoing = bucket(row_dialogue[None], new_slot, frames, device_count, capacity)
    arrived = exchange(outgoing, device_count, capacity)
    prepared = (
        jnp.swapaxes(intersection_cache, 0, 1),
        jnp.swapaxes(history_cache, 0, 1),
        up_bias[None],
        dilated_bias[None],
        project_bias[None],
    )
    arrived, prepared = lax.optimization_barrier((arrived, prepared))
    carried, history, up_bias, dilated_bias, project_bias = prepared
    forwarded, tags = forward(arrived, new_slot, 2 * channels, capacity)
    arrived_caches = exchange(forwarded, device_count, capacity)
    upsampled = decode(
        arrived, carried, history, up_weight, up_bias, dilated_weight, dilated_bias, project_weight, project_bias
    )
    next_intersection, next_history = caches(arrived_caches, tags, up_weight, up_bias, local_count, stride, past)
    return (upsampled, next_intersection, next_history)


def solution(mesh):
    split = P(AXES)
    in_specs = (split,) * 5 + (P(),) * 6
    return jax.shard_map(local, mesh=mesh, in_specs=in_specs, out_specs=(split,) * 3, check_vma=False)
```

```python
import jax
import jax.numpy as jnp
from jax import lax
from jax.experimental import pallas as pl
from jax.experimental.pallas import tpu as pltpu
from jax.sharding import PartitionSpec as P

AXES = ("mp", "codec")
BF16 = jnp.bfloat16
F32 = jnp.float32
I32 = jnp.int32
LANES = 128


def elu(v):
    return jnp.maximum(v, jnp.exp(jnp.minimum(v, 0.0)) - 1.0)


def split_index(index, local_count):
    if local_count & (local_count - 1) == 0:
        shift = local_count.bit_length() - 1
        return index >> shift, index & (local_count - 1)
    return lax.div(index, local_count), lax.rem(index, local_count)


def column_of(row):
    n = row.shape[1]
    eye = lax.broadcasted_iota(I32, (n, n), 0) == lax.broadcasted_iota(I32, (n, n), 1)
    return jnp.sum(jnp.where(eye, jnp.broadcast_to(row, (n, n)), 0), axis=1, keepdims=True)


def row_of(column):
    n = column.shape[0]
    eye = lax.broadcasted_iota(I32, (n, n), 0) == lax.broadcasted_iota(I32, (n, n), 1)
    return jnp.sum(jnp.where(eye, jnp.broadcast_to(column, (n, n)), 0), axis=0, keepdims=True)


def bucket_selector(target_row, local_count, capacity, rows):
    n = target_row.shape[1]
    owner, within = split_index(target_row, local_count)
    owner_column = column_of(owner)
    earlier = lax.broadcasted_iota(I32, (n, n), 0) < lax.broadcasted_iota(I32, (n, n), 1)
    same = (owner_column == owner) & earlier
    rank = jnp.sum(same.astype(I32), axis=0, keepdims=True)
    position = owner * capacity + rank
    chosen = lax.broadcasted_iota(I32, (rows, n), 0) == position
    slots = local_count + jnp.sum(jnp.where(chosen, within - local_count, 0), axis=1, keepdims=True)
    return chosen.astype(F32).astype(BF16), slots


def settle_selector(slots_column, local_count):
    rows = slots_column.shape[0]
    slots = row_of(slots_column)
    chosen = lax.broadcasted_iota(I32, (local_count, rows), 0) == slots
    return chosen.astype(F32).astype(BF16)


def pick(selector, rows):
    return jnp.dot(selector, rows, preferred_element_type=F32).astype(BF16)


def slot_lanes(slots, rows):
    return jnp.broadcast_to(slots.astype(F32), (rows, LANES))


def turner(outer, inner):
    n = outer * inner
    target = lax.broadcasted_iota(I32, (n, n), 0)
    origin = lax.broadcasted_iota(I32, (n, n), 1)
    high, low = split_index(target, inner)
    wanted = low * outer + high
    return (origin == wanted).astype(F32).astype(BF16)


def bucket_kernel(
    target_ref, later_ref, frames_ref, out_ref, landed_ref, active_ref, ready_ref, in_sems, out_sems, *, local_count, capacity
):
    rows, total = ready_ref.shape
    frame_count, channels = landed_ref.shape[1:]
    width = frame_count * channels
    chunks = in_sems.shape[0]
    part = local_count // chunks

    def arrive(n):
        some = pl.ds(n * part, part)
        return pltpu.make_async_copy(frames_ref.at[some], landed_ref.at[some], in_sems.at[n])

    def leave(n):
        some = pl.ds(n * channels, channels if n < frame_count else total - width)
        return pltpu.make_async_copy(ready_ref.at[:, some], out_ref.at[:, some], out_sems.at[n])

    for n in range(chunks):
        arrive(n).start()
    selector, slots = bucket_selector(target_ref[...], local_count, capacity, rows)
    _, later_slots = bucket_selector(later_ref[...], local_count, capacity, rows)
    lane = lax.broadcasted_iota(I32, (rows, LANES), 1)
    tags = jnp.where(lane == 0, slot_lanes(slots, rows), slot_lanes(later_slots, rows))
    ready_ref[:, width:] = tags.astype(BF16)
    leave(frame_count).start()
    number = lax.broadcasted_iota(I32, (rows, local_count), 1) + 1
    origin = jnp.sum(jnp.where(selector.astype(F32) > 0, number, 0), axis=1, keepdims=True) - 1
    for n in range(chunks):
        arrive(n).wait()
        some = landed_ref[n * part : (n + 1) * part].astype(F32).reshape(part * frame_count, channels)
        active_ref[n * part * frame_count : (n + 1) * part * frame_count] = elu(some).astype(BF16)
    column = lax.broadcasted_iota(I32, (rows, local_count * frame_count), 1)
    for t in range(frame_count):
        chosen = (column == origin * frame_count + t).astype(F32).astype(BF16)
        ready_ref[:, t * channels : (t + 1) * channels] = pick(chosen, active_ref[...])
        leave(t).start()
    for n in range(frame_count + 1):
        leave(n).wait()


def forward_kernel(arrived_ref, target_ref, out_ref, tags_ref, *, local_count, capacity):
    rows = out_ref.shape[0]
    width = out_ref.shape[1]
    skip = arrived_ref.shape[1] - LANES - width
    tags = arrived_ref[:, skip + width :]
    tags_ref[...] = tags
    settle = settle_selector(tags.astype(F32)[:, :1].astype(I32), local_count)
    selector, _ = bucket_selector(target_ref[...], local_count, capacity, rows)
    selector = pick(selector, settle)
    half = width // 2
    for n in range(2):
        lanes = slice(skip + n * half, skip + (n + 1) * half)
        out_ref[:, n * half : (n + 1) * half] = pick(selector, arrived_ref[:, lanes])


def decode_kernel(
    arrived_ref,
    weight_ref,
    carried_away_ref,
    history_ref,
    up_bias_ref,
    dilated_away_ref,
    dilated_bias_ref,
    project_away_ref,
    project_bias_ref,
    out_ref,
    active_ref,
    section_ref,
    lifted_ref,
    held_ref,
    carried_ref,
    dilated_ref,
    project_ref,
    ready_ref,
    sems,
    other_sems,
    out_sems,
    *,
    stride,
    block,
):
    frame_count, local_count, channels = active_ref.shape
    hidden = up_bias_ref.shape[1]
    past = history_ref.shape[0]
    taps = past + 1
    length = frame_count * stride

    def fetch(tap):
        columns = pl.ds(pl.multiple_of(tap * hidden, LANES), hidden)
        return pltpu.make_async_copy(weight_ref.at[:, columns], held_ref.at[tap], sems.at[tap])

    def leave(n):
        some = pl.ds(pl.multiple_of(n * block, block), block)
        return pltpu.make_async_copy(ready_ref.at[some], out_ref.at[some], out_sems.at[n])

    carried_copy = pltpu.make_async_copy(carried_away_ref, carried_ref, other_sems.at[0])
    dilated_copy = pltpu.make_async_copy(dilated_away_ref, dilated_ref, other_sems.at[1])
    project_copy = pltpu.make_async_copy(project_away_ref, project_ref, other_sems.at[2])
    ahead = min(2, stride)
    fetch(0).start()
    fetch(stride).start()
    carried_copy.start()
    for s in range(1, ahead):
        fetch(s).start()
        fetch(stride + s).start()

    lifted_ref[0:past] = elu(history_ref[...].astype(F32)).astype(BF16)
    width = frame_count * channels
    settle = settle_selector(arrived_ref[:, width:].astype(F32)[:, :1].astype(I32), local_count)
    for t in range(frame_count):
        active_ref[t] = pick(settle, arrived_ref[:, t * channels : (t + 1) * channels])
    tile = 16
    turn = turner(tile, tile)
    carried_copy.wait()

    def lift(s, _):
        @pl.when(s + ahead < stride)
        def _():
            fetch(s + ahead).start()
            fetch(stride + s + ahead).start()

        @pl.when(s == stride - ahead)
        def _():
            dilated_copy.start()
            project_copy.start()

        fetch(s).wait()
        fetch(stride + s).wait()
        active = active_ref[...].reshape(frame_count * local_count, channels)
        first = jnp.dot(active, held_ref[s], preferred_element_type=F32)
        second = jnp.dot(active, held_ref[stride + s], preferred_element_type=F32)
        bias = up_bias_ref[...].astype(F32)
        for t in range(frame_count):
            now = first[t * local_count : (t + 1) * local_count]
            if t == 0:
                before = carried_ref[s].astype(F32)
            else:
                before = second[(t - 1) * local_count : t * local_count]
            section = (now + before + bias).astype(BF16)
            section_ref[t * stride + s] = section
            lifted_ref[past + t * stride + s] = elu(section.astype(F32)).astype(BF16)
        return 0

    lax.fori_loop(0, stride, lift, 0)
    dilated_copy.wait()
    project_copy.wait()

    def refine(n, _):
        start = pl.multiple_of(n * block, block)
        window = jnp.concatenate(
            [
                lifted_ref[k : k + length, pl.ds(start, block), :].reshape(length * block, hidden)
                for k in range(taps)
            ],
            axis=-1,
        )
        inner = jnp.dot(window, dilated_ref[...], preferred_element_type=F32) + dilated_bias_ref[...].astype(F32)
        inner = elu(inner).astype(BF16)
        branch = jnp.dot(inner, project_ref[...], preferred_element_type=F32) + project_bias_ref[...].astype(F32)
        section = section_ref[:, pl.ds(start, block), :].reshape(length * block, hidden)
        result = (section.astype(F32) + branch).astype(BF16).reshape(length, block, hidden)
        for g in range(0, block, tile):
            for j in range(0, length, tile):
                turned = pick(turn, result[j : j + tile, g : g + tile].reshape(tile * tile, hidden))
                ready_ref[pl.ds(start + g, tile), j : j + tile, :] = turned.reshape(tile, tile, hidden)
        leave(n).start()
        return 0

    lax.fori_loop(0, local_count // block, refine, 0)
    for n in range(local_count // block):
        leave(n).wait()


def caches_kernel(
    arrived_ref, tags_ref, weight_ref, up_bias_ref, inter_ref, hist_ref, kept_ref, held_ref, sems, *, stride, past
):
    local_count = inter_ref.shape[0]
    channels, hidden = held_ref.shape[1:]

    def fetch(n):
        tap = stride + n if n < stride else n - past
        return pltpu.make_async_copy(weight_ref.at[:, pl.ds(tap * hidden, hidden)], held_ref.at[n], sems.at[n])

    order = [stride - past + j for j in range(past)] + [stride + j for j in range(past)] + list(range(stride - past))
    ahead = 5
    for n in order[:ahead]:
        fetch(n).start()
    settle = settle_selector(tags_ref[...].astype(F32)[:, 1:2].astype(I32), local_count)
    before, last = [pick(settle, arrived_ref[:, n * channels : (n + 1) * channels]) for n in range(2)]
    group = 256 // stride
    turn = turner(group, stride)
    turn_past = turner(local_count, past)
    sections = []
    for i, n in enumerate(order):
        fetch(n).wait()
        if i + ahead < len(order):
            fetch(order[i + ahead]).start()
        if n < stride:
            kept_ref[n] = jnp.dot(last, held_ref[n], preferred_element_type=F32).astype(BF16)
        else:
            section = (
                jnp.dot(last, held_ref[n], preferred_element_type=F32)
                + jnp.dot(before, held_ref[n - past], preferred_element_type=F32)
                + up_bias_ref[...].astype(F32)
            )
            sections.append(section.astype(BF16))
            if len(sections) == past:
                turned = jnp.dot(turn_past, jnp.concatenate(sections, axis=0), preferred_element_type=F32)
                hist_ref[...] = turned.reshape(local_count, past, hidden).astype(BF16)
    for g in range(0, local_count, group):
        rows = kept_ref[:, g : g + group, :].reshape(stride * group, hidden)
        turned = jnp.dot(turn, rows, preferred_element_type=F32)
        inter_ref[g : g + group] = turned.reshape(group, stride, hidden).astype(BF16)


def exchange(rows, device_count, capacity):
    width = rows.shape[1]
    moved = lax.all_to_all(
        rows.reshape(device_count, capacity, width), AXES, split_axis=0, concat_axis=0, tiled=True
    )
    return moved.reshape(device_count * capacity, width)


def room(mebibytes):
    return pltpu.CompilerParams(vmem_limit_bytes=mebibytes * 1024 * 1024)


NEAR = pl.BlockSpec(memory_space=pltpu.VMEM)
AWAY = pl.BlockSpec(memory_space=pl.ANY)


def far(array):
    return pltpu.with_memory_space_constraint(array, pltpu.HBM)


def near(array):
    return pltpu.with_memory_space_constraint(array, pltpu.VMEM)


def whole(shape):
    return pl.BlockSpec(shape, lambda i: (0,) * len(shape))


def bucket(row_dialogue, new_slot, frames, device_count, capacity):
    local_count, frame_count, channels = frames.shape
    rows = device_count * capacity
    total = frame_count * channels + LANES
    chunks = 4
    return pl.pallas_call(
        lambda *refs: bucket_kernel(*refs, local_count=local_count, capacity=capacity),
        in_specs=[NEAR, NEAR, AWAY],
        out_specs=AWAY,
        out_shape=pltpu.HBM((rows, total), BF16),
        scratch_shapes=[
            pltpu.VMEM(frames.shape, BF16),
            pltpu.VMEM((local_count * frame_count, channels), BF16),
            pltpu.VMEM((rows, total), BF16),
            pltpu.SemaphoreType.DMA((chunks,)),
            pltpu.SemaphoreType.DMA((frame_count + 1,)),
        ],
        compiler_params=room(24),
        name="bucket",
    )(far(row_dialogue), far(new_slot), far(frames))


def forward(arrived, new_slot, width, capacity):
    local_count = new_slot.shape[1]
    rows = arrived.shape[0]
    return pl.pallas_call(
        lambda *refs: forward_kernel(*refs, local_count=local_count, capacity=capacity),
        out_shape=(
            pltpu.HBM((rows, width), BF16),
            pltpu.VMEM((rows, LANES), BF16),
        ),
        compiler_params=room(40),
        name="forward",
    )(near(arrived), new_slot)


def decode(
    arrived, carried, history, up_weight, up_bias, dilated_weight, dilated_bias, project_weight, project_bias,
):
    channels = up_weight.shape[0]
    frame_count = arrived.shape[1] // channels
    stride, local_count, hidden = carried.shape
    past = history.shape[0]
    length = frame_count * stride
    block = 32
    return pl.pallas_call(
        lambda *refs: decode_kernel(*refs, stride=stride, block=block),
        in_specs=[NEAR, AWAY, AWAY, NEAR, NEAR, AWAY, NEAR, AWAY, NEAR],
        out_specs=AWAY,
        out_shape=pltpu.HBM((local_count, length, hidden), BF16),
        scratch_shapes=[
            pltpu.VMEM((frame_count, local_count, channels), BF16),
            pltpu.VMEM((length, local_count, hidden), BF16),
            pltpu.VMEM((past + length, local_count, hidden), BF16),
            pltpu.VMEM((2 * stride, channels, hidden), BF16),
            pltpu.VMEM(carried.shape, BF16),
            pltpu.VMEM(dilated_weight.shape, BF16),
            pltpu.VMEM(project_weight.shape, BF16),
            pltpu.VMEM((local_count, length, hidden), BF16),
            pltpu.SemaphoreType.DMA((2 * stride,)),
            pltpu.SemaphoreType.DMA((3,)),
            pltpu.SemaphoreType.DMA((local_count // block,)),
        ],
        compiler_params=room(48),
        name="decode",
    )(
        near(arrived),
        far(up_weight),
        far(carried),
        history,
        up_bias,
        far(dilated_weight),
        dilated_bias,
        far(project_weight),
        project_bias,
    )


def caches(arrived, tags, up_weight, up_bias, local_count, stride, past):
    channels = up_weight.shape[0]
    hidden = up_bias.shape[1]
    return pl.pallas_call(
        lambda *refs: caches_kernel(*refs, stride=stride, past=past),
        in_specs=[NEAR, NEAR, AWAY, NEAR],
        out_shape=(
            jax.ShapeDtypeStruct((local_count, stride, hidden), BF16),
            jax.ShapeDtypeStruct((local_count, past, hidden), BF16),
        ),
        scratch_shapes=[
            pltpu.VMEM((stride, local_count, hidden), BF16),
            pltpu.VMEM((stride + past, channels, hidden), BF16),
            pltpu.SemaphoreType.DMA((stride + past,)),
        ],
        compiler_params=room(24),
        name="caches",
    )(near(arrived), near(tags), far(up_weight), up_bias)


def local(
    frames,
    row_dialogue,
    intersection_cache,
    history_cache,
    new_slot,
    up_weight,
    up_bias,
    dilated_weight,
    dilated_bias,
    project_weight,
    project_bias,
):
    local_count, frame_count, channels = frames.shape
    stride, hidden = intersection_cache.shape[1:]
    past = history_cache.shape[1]
    device_count = lax.axis_size("mp") * lax.axis_size("codec")
    capacity = 2 * local_count // device_count
    new_slot = new_slot[None]

    outgoing = bucket(row_dialogue[None], new_slot, frames, device_count, capacity)
    arrived = exchange(outgoing, device_count, capacity)
    prepared = (
        jnp.swapaxes(intersection_cache, 0, 1),
        jnp.swapaxes(history_cache, 0, 1),
        up_bias[None],
        dilated_bias[None],
        project_bias[None],
    )
    arrived, prepared = lax.optimization_barrier((arrived, prepared))
    carried, history, up_bias, dilated_bias, project_bias = prepared
    forwarded, tags = forward(arrived, new_slot, 2 * channels, capacity)
    arrived_caches = exchange(forwarded, device_count, capacity)
    upsampled = decode(
        arrived, carried, history, up_weight, up_bias, dilated_weight, dilated_bias, project_weight, project_bias
    )
    next_intersection, next_history = caches(arrived_caches, tags, up_weight, up_bias, local_count, stride, past)
    return (upsampled, next_intersection, next_history)


def solution(mesh):
    split = P(AXES)
    in_specs = (split,) * 5 + (P(),) * 6
    return jax.shard_map(local, mesh=mesh, in_specs=in_specs, out_specs=(split,) * 3, check_vma=False)
```

```python
import jax
import jax.numpy as jnp
from jax import lax
from jax.experimental import pallas as pl
from jax.experimental.pallas import tpu as pltpu
from jax.sharding import PartitionSpec as P

AXES = ("mp", "codec")
BF16 = jnp.bfloat16
F32 = jnp.float32
I32 = jnp.int32
LANES = 128


def elu(v):
    return jnp.maximum(v, jnp.exp(jnp.minimum(v, 0.0)) - 1.0)


def split_index(index, local_count):
    if local_count & (local_count - 1) == 0:
        shift = local_count.bit_length() - 1
        return index >> shift, index & (local_count - 1)
    return lax.div(index, local_count), lax.rem(index, local_count)


def column_of(row):
    n = row.shape[1]
    eye = lax.broadcasted_iota(I32, (n, n), 0) == lax.broadcasted_iota(I32, (n, n), 1)
    return jnp.sum(jnp.where(eye, jnp.broadcast_to(row, (n, n)), 0), axis=1, keepdims=True)


def row_of(column):
    n = column.shape[0]
    eye = lax.broadcasted_iota(I32, (n, n), 0) == lax.broadcasted_iota(I32, (n, n), 1)
    return jnp.sum(jnp.where(eye, jnp.broadcast_to(column, (n, n)), 0), axis=0, keepdims=True)


def bucket_selector(target_row, local_count, capacity, rows):
    n = target_row.shape[1]
    owner, within = split_index(target_row, local_count)
    owner_column = column_of(owner)
    earlier = lax.broadcasted_iota(I32, (n, n), 0) < lax.broadcasted_iota(I32, (n, n), 1)
    same = (owner_column == owner) & earlier
    rank = jnp.sum(same.astype(I32), axis=0, keepdims=True)
    position = owner * capacity + rank
    chosen = lax.broadcasted_iota(I32, (rows, n), 0) == position
    slots = local_count + jnp.sum(jnp.where(chosen, within - local_count, 0), axis=1, keepdims=True)
    return chosen.astype(F32).astype(BF16), slots


def settle_selector(slots_column, local_count):
    rows = slots_column.shape[0]
    slots = row_of(slots_column)
    chosen = lax.broadcasted_iota(I32, (local_count, rows), 0) == slots
    return chosen.astype(F32).astype(BF16)


def pick(selector, rows):
    return jnp.dot(selector, rows, preferred_element_type=F32).astype(BF16)


def slot_lanes(slots, rows):
    return jnp.broadcast_to(slots.astype(F32), (rows, LANES))


def turner(outer, inner):
    n = outer * inner
    target = lax.broadcasted_iota(I32, (n, n), 0)
    origin = lax.broadcasted_iota(I32, (n, n), 1)
    high, low = split_index(target, inner)
    wanted = low * outer + high
    return (origin == wanted).astype(F32).astype(BF16)


def bucket_kernel(target_ref, later_ref, frames_ref, out_ref, ready_ref, sems, *, local_count, capacity):
    rows, total = ready_ref.shape
    width = frames_ref.shape[1]
    parts = sems.shape[0] - 1
    part = width // parts

    def leave(n):
        some = pl.ds(n * part, part if n < parts else total - width)
        return pltpu.make_async_copy(ready_ref.at[:, some], out_ref.at[:, some], sems.at[n])

    selector, slots = bucket_selector(target_ref[...], local_count, capacity, rows)
    for n in range(parts):
        lanes = slice(n * part, (n + 1) * part)
        ready_ref[:, lanes] = pick(selector, elu(frames_ref[:, lanes].astype(F32)).astype(BF16))
        leave(n).start()
    _, later_slots = bucket_selector(later_ref[...], local_count, capacity, rows)
    lane = lax.broadcasted_iota(I32, (rows, LANES), 1)
    tags = jnp.where(lane == 0, slot_lanes(slots, rows), slot_lanes(later_slots, rows))
    ready_ref[:, width:] = tags.astype(BF16)
    leave(parts).start()
    for n in range(parts + 1):
        leave(n).wait()


def select_kernel(target_ref, out_ref, *, local_count, capacity):
    out_ref[...], _ = bucket_selector(target_ref[...], local_count, capacity, out_ref.shape[0])


def forward_kernel(arrived_ref, selector_ref, out_ref, tags_ref, ready_ref, sems):
    width = ready_ref.shape[1]
    local_count = selector_ref.shape[1]
    skip = arrived_ref.shape[1] - LANES - width
    parts = sems.shape[0]
    part = width // parts

    def leave(n):
        some = pl.ds(n * part, part)
        return pltpu.make_async_copy(ready_ref.at[:, some], out_ref.at[:, some], sems.at[n])

    tags = arrived_ref[:, skip + width :]
    tags_ref[...] = tags
    settle = settle_selector(tags.astype(F32)[:, :1].astype(I32), local_count)
    selector = pick(selector_ref[...], settle)
    for n in range(parts):
        lanes = slice(skip + n * part, skip + (n + 1) * part)
        ready_ref[:, n * part : (n + 1) * part] = pick(selector, arrived_ref[:, lanes])
        leave(n).start()
    for n in range(parts):
        leave(n).wait()


def decode_kernel(
    arrived_ref,
    weight_ref,
    carried_away_ref,
    history_ref,
    up_bias_ref,
    dilated_away_ref,
    dilated_bias_ref,
    project_away_ref,
    project_bias_ref,
    out_ref,
    active_ref,
    section_ref,
    lifted_ref,
    held_ref,
    carried_ref,
    dilated_ref,
    project_ref,
    ready_ref,
    sems,
    other_sems,
    out_sems,
    *,
    stride,
    block,
):
    frame_count, local_count, channels = active_ref.shape
    hidden = up_bias_ref.shape[1]
    past = history_ref.shape[0]
    taps = past + 1
    length = frame_count * stride

    def fetch(tap):
        columns = pl.ds(pl.multiple_of(tap * hidden, LANES), hidden)
        return pltpu.make_async_copy(weight_ref.at[:, columns], held_ref.at[tap], sems.at[tap])

    def leave(n):
        some = pl.ds(pl.multiple_of(n * block, block), block)
        return pltpu.make_async_copy(ready_ref.at[some], out_ref.at[some], out_sems.at[n])

    carried_copy = pltpu.make_async_copy(carried_away_ref, carried_ref, other_sems.at[0])
    dilated_copy = pltpu.make_async_copy(dilated_away_ref, dilated_ref, other_sems.at[1])
    project_copy = pltpu.make_async_copy(project_away_ref, project_ref, other_sems.at[2])
    ahead = min(2, stride)
    fetch(0).start()
    fetch(stride).start()
    carried_copy.start()
    for s in range(1, ahead):
        fetch(s).start()
        fetch(stride + s).start()

    lifted_ref[0:past] = elu(history_ref[...].astype(F32)).astype(BF16)
    width = frame_count * channels
    settle = settle_selector(arrived_ref[:, width:].astype(F32)[:, :1].astype(I32), local_count)
    for t in range(frame_count):
        active_ref[t] = pick(settle, arrived_ref[:, t * channels : (t + 1) * channels])
    tile = 16
    turn = turner(tile, tile)
    carried_copy.wait()

    def lift(s, _):
        @pl.when(s + ahead < stride)
        def _():
            fetch(s + ahead).start()
            fetch(stride + s + ahead).start()

        @pl.when(s == stride - ahead)
        def _():
            dilated_copy.start()
            project_copy.start()

        fetch(s).wait()
        fetch(stride + s).wait()
        active = active_ref[...].reshape(frame_count * local_count, channels)
        first = jnp.dot(active, held_ref[s], preferred_element_type=F32)
        second = jnp.dot(active, held_ref[stride + s], preferred_element_type=F32)
        bias = up_bias_ref[...].astype(F32)
        for t in range(frame_count):
            now = first[t * local_count : (t + 1) * local_count]
            if t == 0:
                before = carried_ref[s].astype(F32)
            else:
                before = second[(t - 1) * local_count : t * local_count]
            section = (now + before + bias).astype(BF16)
            section_ref[t * stride + s] = section
            lifted_ref[past + t * stride + s] = elu(section.astype(F32)).astype(BF16)
        return 0

    lax.fori_loop(0, stride, lift, 0)
    dilated_copy.wait()
    project_copy.wait()

    def refine(n, _):
        start = pl.multiple_of(n * block, block)
        window = jnp.concatenate(
            [
                lifted_ref[k : k + length, pl.ds(start, block), :].reshape(length * block, hidden)
                for k in range(taps)
            ],
            axis=-1,
        )
        inner = jnp.dot(window, dilated_ref[...], preferred_element_type=F32) + dilated_bias_ref[...].astype(F32)
        inner = elu(inner).astype(BF16)
        branch = jnp.dot(inner, project_ref[...], preferred_element_type=F32) + project_bias_ref[...].astype(F32)
        section = section_ref[:, pl.ds(start, block), :].reshape(length * block, hidden)
        result = (section.astype(F32) + branch).astype(BF16).reshape(length, block, hidden)
        for g in range(0, block, tile):
            for j in range(0, length, tile):
                turned = pick(turn, result[j : j + tile, g : g + tile].reshape(tile * tile, hidden))
                ready_ref[pl.ds(start + g, tile), j : j + tile, :] = turned.reshape(tile, tile, hidden)
        leave(n).start()
        return 0

    lax.fori_loop(0, local_count // block, refine, 0)
    for n in range(local_count // block):
        leave(n).wait()


def caches_kernel(
    arrived_ref, tags_ref, weight_ref, up_bias_ref, inter_ref, hist_ref, kept_ref, held_ref, sems, *, stride, past
):
    local_count = inter_ref.shape[0]
    channels, hidden = held_ref.shape[1:]

    def fetch(n):
        tap = stride + n if n < stride else n - past
        return pltpu.make_async_copy(weight_ref.at[:, pl.ds(tap * hidden, hidden)], held_ref.at[n], sems.at[n])

    order = [stride - past + j for j in range(past)] + [stride + j for j in range(past)] + list(range(stride - past))
    ahead = 5
    for n in order[:ahead]:
        fetch(n).start()
    settle = settle_selector(tags_ref[...].astype(F32)[:, 1:2].astype(I32), local_count)
    before, last = [pick(settle, arrived_ref[:, n * channels : (n + 1) * channels]) for n in range(2)]
    group = 256 // stride
    turn = turner(group, stride)
    turn_past = turner(local_count, past)
    sections = []
    for i, n in enumerate(order):
        fetch(n).wait()
        if i + ahead < len(order):
            fetch(order[i + ahead]).start()
        if n < stride:
            kept_ref[n] = jnp.dot(last, held_ref[n], preferred_element_type=F32).astype(BF16)
        else:
            section = (
                jnp.dot(last, held_ref[n], preferred_element_type=F32)
                + jnp.dot(before, held_ref[n - past], preferred_element_type=F32)
                + up_bias_ref[...].astype(F32)
            )
            sections.append(section.astype(BF16))
            if len(sections) == past:
                turned = jnp.dot(turn_past, jnp.concatenate(sections, axis=0), preferred_element_type=F32)
                hist_ref[...] = turned.reshape(local_count, past, hidden).astype(BF16)
    for g in range(0, local_count, group):
        rows = kept_ref[:, g : g + group, :].reshape(stride * group, hidden)
        turned = jnp.dot(turn, rows, preferred_element_type=F32)
        inter_ref[g : g + group] = turned.reshape(group, stride, hidden).astype(BF16)


def exchange(rows, device_count, capacity):
    width = rows.shape[1]
    moved = lax.all_to_all(
        rows.reshape(device_count, capacity, width), AXES, split_axis=0, concat_axis=0, tiled=True
    )
    return moved.reshape(device_count * capacity, width)


def room(mebibytes):
    return pltpu.CompilerParams(vmem_limit_bytes=mebibytes * 1024 * 1024)


NEAR = pl.BlockSpec(memory_space=pltpu.VMEM)
AWAY = pl.BlockSpec(memory_space=pl.ANY)


def far(array):
    return pltpu.with_memory_space_constraint(array, pltpu.HBM)


def near(array):
    return pltpu.with_memory_space_constraint(array, pltpu.VMEM)


def whole(shape):
    return pl.BlockSpec(shape, lambda i: (0,) * len(shape))


def bucket(row_dialogue, new_slot, frames, device_count, capacity):
    local_count, frame_count, channels = frames.shape
    rows = device_count * capacity
    total = frame_count * channels + LANES
    return pl.pallas_call(
        lambda *refs: bucket_kernel(*refs, local_count=local_count, capacity=capacity),
        in_specs=[NEAR, NEAR, NEAR],
        out_specs=AWAY,
        out_shape=pltpu.HBM((rows, total), BF16),
        scratch_shapes=[
            pltpu.VMEM((rows, total), BF16),
            pltpu.SemaphoreType.DMA((frame_count + 1,)),
        ],
        compiler_params=room(24),
        name="bucket",
    )(far(row_dialogue), far(new_slot), near(frames.reshape(local_count, frame_count * channels)))


def select(target, rows, capacity):
    local_count = target.shape[1]
    return pl.pallas_call(
        lambda *refs: select_kernel(*refs, local_count=local_count, capacity=capacity),
        out_shape=jax.ShapeDtypeStruct((rows, local_count), BF16),
        compiler_params=room(8),
        name="select",
    )(target)


def forward(arrived, selector, width):
    rows = arrived.shape[0]
    parts = 4
    return pl.pallas_call(
        forward_kernel,
        in_specs=[NEAR, NEAR],
        out_specs=(AWAY, NEAR),
        out_shape=(pltpu.HBM((rows, width), BF16), pltpu.VMEM((rows, LANES), BF16)),
        scratch_shapes=[pltpu.VMEM((rows, width), BF16), pltpu.SemaphoreType.DMA((parts,))],
        compiler_params=room(16),
        name="forward",
    )(near(arrived), near(selector))


def decode(
    arrived, carried, history, up_weight, up_bias, dilated_weight, dilated_bias, project_weight, project_bias,
):
    channels = up_weight.shape[0]
    frame_count = arrived.shape[1] // channels
    stride, local_count, hidden = carried.shape
    past = history.shape[0]
    length = frame_count * stride
    block = 32
    return pl.pallas_call(
        lambda *refs: decode_kernel(*refs, stride=stride, block=block),
        in_specs=[NEAR, AWAY, AWAY, NEAR, NEAR, AWAY, NEAR, AWAY, NEAR],
        out_specs=AWAY,
        out_shape=pltpu.HBM((local_count, length, hidden), BF16),
        scratch_shapes=[
            pltpu.VMEM((frame_count, local_count, channels), BF16),
            pltpu.VMEM((length, local_count, hidden), BF16),
            pltpu.VMEM((past + length, local_count, hidden), BF16),
            pltpu.VMEM((2 * stride, channels, hidden), BF16),
            pltpu.VMEM(carried.shape, BF16),
            pltpu.VMEM(dilated_weight.shape, BF16),
            pltpu.VMEM(project_weight.shape, BF16),
            pltpu.VMEM((local_count, length, hidden), BF16),
            pltpu.SemaphoreType.DMA((2 * stride,)),
            pltpu.SemaphoreType.DMA((3,)),
            pltpu.SemaphoreType.DMA((local_count // block,)),
        ],
        compiler_params=room(48),
        name="decode",
    )(
        near(arrived),
        far(up_weight),
        far(carried),
        history,
        up_bias,
        far(dilated_weight),
        dilated_bias,
        far(project_weight),
        project_bias,
    )


def caches(arrived, tags, up_weight, up_bias, local_count, stride, past):
    channels = up_weight.shape[0]
    hidden = up_bias.shape[1]
    return pl.pallas_call(
        lambda *refs: caches_kernel(*refs, stride=stride, past=past),
        in_specs=[NEAR, NEAR, AWAY, NEAR],
        out_shape=(
            jax.ShapeDtypeStruct((local_count, stride, hidden), BF16),
            jax.ShapeDtypeStruct((local_count, past, hidden), BF16),
        ),
        scratch_shapes=[
            pltpu.VMEM((stride, local_count, hidden), BF16),
            pltpu.VMEM((stride + past, channels, hidden), BF16),
            pltpu.SemaphoreType.DMA((stride + past,)),
        ],
        compiler_params=room(24),
        name="caches",
    )(near(arrived), near(tags), far(up_weight), up_bias)


def local(
    frames,
    row_dialogue,
    intersection_cache,
    history_cache,
    new_slot,
    up_weight,
    up_bias,
    dilated_weight,
    dilated_bias,
    project_weight,
    project_bias,
):
    local_count, frame_count, channels = frames.shape
    stride, hidden = intersection_cache.shape[1:]
    past = history_cache.shape[1]
    device_count = lax.axis_size("mp") * lax.axis_size("codec")
    capacity = 2 * local_count // device_count
    new_slot = new_slot[None]

    outgoing = bucket(row_dialogue[None], new_slot, frames, device_count, capacity)
    arrived = exchange(outgoing, device_count, capacity)
    prepared = (
        jnp.swapaxes(intersection_cache, 0, 1),
        jnp.swapaxes(history_cache, 0, 1),
        up_bias[None],
        dilated_bias[None],
        project_bias[None],
        select(new_slot, device_count * capacity, capacity),
    )
    arrived, prepared = lax.optimization_barrier((arrived, prepared))
    carried, history, up_bias, dilated_bias, project_bias, selector = prepared
    forwarded, tags = forward(arrived, selector, 2 * channels)
    arrived_caches = exchange(forwarded, device_count, capacity)
    upsampled = decode(
        arrived, carried, history, up_weight, up_bias, dilated_weight, dilated_bias, project_weight, project_bias
    )
    next_intersection, next_history = caches(arrived_caches, tags, up_weight, up_bias, local_count, stride, past)
    return (upsampled, next_intersection, next_history)


def solution(mesh):
    split = P(AXES)
    in_specs = (split,) * 5 + (P(),) * 6
    return jax.shard_map(local, mesh=mesh, in_specs=in_specs, out_specs=(split,) * 3, check_vma=False)
```

```python
import jax
import jax.numpy as jnp
from jax import lax
from jax.experimental import pallas as pl
from jax.experimental.pallas import tpu as pltpu
from jax.sharding import PartitionSpec as P

AXES = ("mp", "codec")
BF16 = jnp.bfloat16
F32 = jnp.float32
I32 = jnp.int32
LANES = 128


def elu(v):
    return jnp.maximum(v, jnp.exp(jnp.minimum(v, 0.0)) - 1.0)


def split_index(index, local_count):
    if local_count & (local_count - 1) == 0:
        shift = local_count.bit_length() - 1
        return index >> shift, index & (local_count - 1)
    return lax.div(index, local_count), lax.rem(index, local_count)


def column_of(row):
    n = row.shape[1]
    eye = lax.broadcasted_iota(I32, (n, n), 0) == lax.broadcasted_iota(I32, (n, n), 1)
    return jnp.sum(jnp.where(eye, jnp.broadcast_to(row, (n, n)), 0), axis=1, keepdims=True)


def row_of(column):
    n = column.shape[0]
    eye = lax.broadcasted_iota(I32, (n, n), 0) == lax.broadcasted_iota(I32, (n, n), 1)
    return jnp.sum(jnp.where(eye, jnp.broadcast_to(column, (n, n)), 0), axis=0, keepdims=True)


def bucket_selector(target_row, local_count, capacity, rows):
    n = target_row.shape[1]
    owner, within = split_index(target_row, local_count)
    owner_column = column_of(owner)
    earlier = lax.broadcasted_iota(I32, (n, n), 0) < lax.broadcasted_iota(I32, (n, n), 1)
    same = (owner_column == owner) & earlier
    rank = jnp.sum(same.astype(I32), axis=0, keepdims=True)
    position = owner * capacity + rank
    chosen = lax.broadcasted_iota(I32, (rows, n), 0) == position
    slots = local_count + jnp.sum(jnp.where(chosen, within - local_count, 0), axis=1, keepdims=True)
    return chosen.astype(F32).astype(BF16), slots


def settle_selector(slots_column, local_count):
    rows = slots_column.shape[0]
    slots = row_of(slots_column)
    chosen = lax.broadcasted_iota(I32, (local_count, rows), 0) == slots
    return chosen.astype(F32).astype(BF16)


def pick(selector, rows):
    return jnp.dot(selector, rows, preferred_element_type=F32).astype(BF16)


def slot_lanes(slots, rows):
    return jnp.broadcast_to(slots.astype(F32), (rows, LANES))


def activate(selector, rows):
    return elu(jnp.dot(selector, rows, preferred_element_type=F32)).astype(BF16)


def turner(outer, inner):
    n = outer * inner
    target = lax.broadcasted_iota(I32, (n, n), 0)
    origin = lax.broadcasted_iota(I32, (n, n), 1)
    high, low = split_index(target, inner)
    wanted = low * outer + high
    return (origin == wanted).astype(F32).astype(BF16)


def bucket_kernel(target_ref, later_ref, frames_ref, out_ref, ready_ref, sems, *, local_count, capacity):
    rows, total = ready_ref.shape
    width = frames_ref.shape[1]
    parts = sems.shape[0] - 1
    part = width // parts

    def leave(n):
        some = pl.ds(n * part, part if n < parts else total - width)
        return pltpu.make_async_copy(ready_ref.at[:, some], out_ref.at[:, some], sems.at[n])

    selector, slots = bucket_selector(target_ref[...], local_count, capacity, rows)
    for n in range(parts):
        lanes = slice(n * part, (n + 1) * part)
        ready_ref[:, lanes] = pick(selector, frames_ref[:, lanes])
        leave(n).start()
    _, later_slots = bucket_selector(later_ref[...], local_count, capacity, rows)
    lane = lax.broadcasted_iota(I32, (rows, LANES), 1)
    tags = jnp.where(lane == 0, slot_lanes(slots, rows), slot_lanes(later_slots, rows))
    ready_ref[:, width:] = tags.astype(BF16)
    leave(parts).start()
    for n in range(parts + 1):
        leave(n).wait()


def select_kernel(target_ref, out_ref, *, local_count, capacity):
    out_ref[...], _ = bucket_selector(target_ref[...], local_count, capacity, out_ref.shape[0])


def forward_kernel(arrived_ref, selector_ref, out_ref, tags_ref, ready_ref, sems):
    width = ready_ref.shape[1]
    local_count = selector_ref.shape[1]
    skip = arrived_ref.shape[1] - LANES - width
    parts = sems.shape[0]
    part = width // parts

    def leave(n):
        some = pl.ds(n * part, part)
        return pltpu.make_async_copy(ready_ref.at[:, some], out_ref.at[:, some], sems.at[n])

    tags = arrived_ref[:, skip + width :]
    tags_ref[...] = tags
    settle = settle_selector(tags.astype(F32)[:, :1].astype(I32), local_count)
    selector = pick(selector_ref[...], settle)
    for n in range(parts):
        lanes = slice(skip + n * part, skip + (n + 1) * part)
        ready_ref[:, n * part : (n + 1) * part] = pick(selector, arrived_ref[:, lanes])
        leave(n).start()
    for n in range(parts):
        leave(n).wait()


def decode_kernel(
    arrived_ref,
    weight_ref,
    carried_away_ref,
    history_ref,
    up_bias_ref,
    dilated_away_ref,
    dilated_bias_ref,
    project_away_ref,
    project_bias_ref,
    out_ref,
    active_ref,
    section_ref,
    lifted_ref,
    held_ref,
    carried_ref,
    dilated_ref,
    project_ref,
    ready_ref,
    sems,
    other_sems,
    out_sems,
    *,
    stride,
    block,
):
    frame_count, local_count, channels = active_ref.shape
    hidden = up_bias_ref.shape[1]
    past = history_ref.shape[0]
    taps = past + 1
    length = frame_count * stride

    def fetch(tap):
        columns = pl.ds(pl.multiple_of(tap * hidden, LANES), hidden)
        return pltpu.make_async_copy(weight_ref.at[:, columns], held_ref.at[tap], sems.at[tap])

    def leave(n):
        some = pl.ds(pl.multiple_of(n * block, block), block)
        return pltpu.make_async_copy(ready_ref.at[some], out_ref.at[some], out_sems.at[n])

    carried_copy = pltpu.make_async_copy(carried_away_ref, carried_ref, other_sems.at[0])
    dilated_copy = pltpu.make_async_copy(dilated_away_ref, dilated_ref, other_sems.at[1])
    project_copy = pltpu.make_async_copy(project_away_ref, project_ref, other_sems.at[2])
    ahead = min(2, stride)
    fetch(0).start()
    fetch(stride).start()
    carried_copy.start()
    for s in range(1, ahead):
        fetch(s).start()
        fetch(stride + s).start()

    lifted_ref[0:past] = elu(history_ref[...].astype(F32)).astype(BF16)
    width = frame_count * channels
    settle = settle_selector(arrived_ref[:, width:].astype(F32)[:, :1].astype(I32), local_count)
    for t in range(frame_count):
        active_ref[t] = activate(settle, arrived_ref[:, t * channels : (t + 1) * channels])
    tile = 16
    turn = turner(tile, tile)
    carried_copy.wait()

    def lift(s, _):
        @pl.when(s + ahead < stride)
        def _():
            fetch(s + ahead).start()
            fetch(stride + s + ahead).start()

        @pl.when(s == stride - ahead)
        def _():
            dilated_copy.start()
            project_copy.start()

        fetch(s).wait()
        fetch(stride + s).wait()
        active = active_ref[...].reshape(frame_count * local_count, channels)
        first = jnp.dot(active, held_ref[s], preferred_element_type=F32)
        second = jnp.dot(active, held_ref[stride + s], preferred_element_type=F32)
        bias = up_bias_ref[...].astype(F32)
        for t in range(frame_count):
            now = first[t * local_count : (t + 1) * local_count]
            if t == 0:
                before = carried_ref[s].astype(F32)
            else:
                before = second[(t - 1) * local_count : t * local_count]
            section = (now + before + bias).astype(BF16)
            section_ref[t * stride + s] = section
            lifted_ref[past + t * stride + s] = elu(section.astype(F32)).astype(BF16)
        return 0

    lax.fori_loop(0, stride, lift, 0)
    dilated_copy.wait()
    project_copy.wait()

    def refine(n, _):
        start = pl.multiple_of(n * block, block)
        window = jnp.concatenate(
            [
                lifted_ref[k : k + length, pl.ds(start, block), :].reshape(length * block, hidden)
                for k in range(taps)
            ],
            axis=-1,
        )
        inner = jnp.dot(window, dilated_ref[...], preferred_element_type=F32) + dilated_bias_ref[...].astype(F32)
        inner = elu(inner).astype(BF16)
        branch = jnp.dot(inner, project_ref[...], preferred_element_type=F32) + project_bias_ref[...].astype(F32)
        section = section_ref[:, pl.ds(start, block), :].reshape(length * block, hidden)
        result = (section.astype(F32) + branch).astype(BF16).reshape(length, block, hidden)
        for g in range(0, block, tile):
            for j in range(0, length, tile):
                turned = pick(turn, result[j : j + tile, g : g + tile].reshape(tile * tile, hidden))
                ready_ref[pl.ds(start + g, tile), j : j + tile, :] = turned.reshape(tile, tile, hidden)
        leave(n).start()
        return 0

    lax.fori_loop(0, local_count // block, refine, 0)
    for n in range(local_count // block):
        leave(n).wait()


def caches_kernel(
    arrived_ref, tags_ref, weight_ref, up_bias_ref, inter_ref, hist_ref, kept_ref, held_ref, sems, *, stride, past
):
    local_count = inter_ref.shape[0]
    channels, hidden = held_ref.shape[1:]

    def fetch(n):
        tap = stride + n if n < stride else n - past
        return pltpu.make_async_copy(weight_ref.at[:, pl.ds(tap * hidden, hidden)], held_ref.at[n], sems.at[n])

    order = [stride + j for j in range(past)] + [stride - past + j for j in range(past)] + list(range(stride - past))
    for n in order:
        fetch(n).start()
    settle = settle_selector(tags_ref[...].astype(F32)[:, 1:2].astype(I32), local_count)
    last, before = [activate(settle, arrived_ref[:, n * channels : (n + 1) * channels]) for n in (1, 0)]
    both = jnp.concatenate([last, before], axis=0)
    bias = up_bias_ref[...].astype(F32)
    sections = []
    for n in order:
        fetch(n).wait()
        if n >= stride:
            sections.append(jnp.dot(last, held_ref[n], preferred_element_type=F32) + bias)
        elif n >= stride - past:
            seconds = jnp.dot(both, held_ref[n], preferred_element_type=F32)
            kept_ref[n] = seconds[:local_count].astype(BF16)
            sections[n - stride + past] += seconds[local_count:]
        else:
            kept_ref[n] = jnp.dot(last, held_ref[n], preferred_element_type=F32).astype(BF16)
    group = 256 // stride
    turn = turner(group, stride)
    for g in range(0, local_count, group):
        rows = kept_ref[:, g : g + group, :].reshape(stride * group, hidden)
        turned = jnp.dot(turn, rows, preferred_element_type=F32)
        inter_ref[g : g + group] = turned.reshape(group, stride, hidden).astype(BF16)
    sections = jnp.concatenate([section.astype(BF16) for section in sections], axis=0)
    turned = jnp.dot(turner(local_count, past), sections, preferred_element_type=F32)
    hist_ref[...] = turned.reshape(local_count, past, hidden).astype(BF16)


def exchange(rows, device_count, capacity):
    width = rows.shape[1]
    moved = lax.all_to_all(
        rows.reshape(device_count, capacity, width), AXES, split_axis=0, concat_axis=0, tiled=True
    )
    return moved.reshape(device_count * capacity, width)


def room(mebibytes):
    return pltpu.CompilerParams(vmem_limit_bytes=mebibytes * 1024 * 1024)


NEAR = pl.BlockSpec(memory_space=pltpu.VMEM)
AWAY = pl.BlockSpec(memory_space=pl.ANY)


def far(array):
    return pltpu.with_memory_space_constraint(array, pltpu.HBM)


def near(array):
    return pltpu.with_memory_space_constraint(array, pltpu.VMEM)


def whole(shape):
    return pl.BlockSpec(shape, lambda i: (0,) * len(shape))


def bucket(row_dialogue, new_slot, frames, device_count, capacity):
    local_count, frame_count, channels = frames.shape
    rows = device_count * capacity
    total = frame_count * channels + LANES
    return pl.pallas_call(
        lambda *refs: bucket_kernel(*refs, local_count=local_count, capacity=capacity),
        in_specs=[NEAR, NEAR, NEAR],
        out_specs=AWAY,
        out_shape=pltpu.HBM((rows, total), BF16),
        scratch_shapes=[
            pltpu.VMEM((rows, total), BF16),
            pltpu.SemaphoreType.DMA((frame_count + 1,)),
        ],
        compiler_params=room(24),
        name="bucket",
    )(far(row_dialogue), far(new_slot), near(frames.reshape(local_count, frame_count * channels)))


def select(target, rows, capacity):
    local_count = target.shape[1]
    return pl.pallas_call(
        lambda *refs: select_kernel(*refs, local_count=local_count, capacity=capacity),
        out_shape=jax.ShapeDtypeStruct((rows, local_count), BF16),
        compiler_params=room(8),
        name="select",
    )(target)


def forward(arrived, selector, width):
    rows = arrived.shape[0]
    parts = 4
    return pl.pallas_call(
        forward_kernel,
        in_specs=[NEAR, NEAR],
        out_specs=(AWAY, NEAR),
        out_shape=(pltpu.HBM((rows, width), BF16), pltpu.VMEM((rows, LANES), BF16)),
        scratch_shapes=[pltpu.VMEM((rows, width), BF16), pltpu.SemaphoreType.DMA((parts,))],
        compiler_params=room(16),
        name="forward",
    )(near(arrived), near(selector))


def decode(
    arrived, carried, history, up_weight, up_bias, dilated_weight, dilated_bias, project_weight, project_bias,
):
    channels = up_weight.shape[0]
    frame_count = arrived.shape[1] // channels
    stride, local_count, hidden = carried.shape
    past = history.shape[0]
    length = frame_count * stride
    block = 32
    return pl.pallas_call(
        lambda *refs: decode_kernel(*refs, stride=stride, block=block),
        in_specs=[NEAR, AWAY, AWAY, NEAR, NEAR, AWAY, NEAR, AWAY, NEAR],
        out_specs=AWAY,
        out_shape=pltpu.HBM((local_count, length, hidden), BF16),
        scratch_shapes=[
            pltpu.VMEM((frame_count, local_count, channels), BF16),
            pltpu.VMEM((length, local_count, hidden), BF16),
            pltpu.VMEM((past + length, local_count, hidden), BF16),
            pltpu.VMEM((2 * stride, channels, hidden), BF16),
            pltpu.VMEM(carried.shape, BF16),
            pltpu.VMEM(dilated_weight.shape, BF16),
            pltpu.VMEM(project_weight.shape, BF16),
            pltpu.VMEM((local_count, length, hidden), BF16),
            pltpu.SemaphoreType.DMA((2 * stride,)),
            pltpu.SemaphoreType.DMA((3,)),
            pltpu.SemaphoreType.DMA((local_count // block,)),
        ],
        compiler_params=room(48),
        name="decode",
    )(
        near(arrived),
        far(up_weight),
        far(carried),
        history,
        up_bias,
        far(dilated_weight),
        dilated_bias,
        far(project_weight),
        project_bias,
    )


def caches(arrived, tags, up_weight, up_bias, local_count, stride, past):
    channels = up_weight.shape[0]
    hidden = up_bias.shape[1]
    return pl.pallas_call(
        lambda *refs: caches_kernel(*refs, stride=stride, past=past),
        in_specs=[NEAR, NEAR, AWAY, NEAR],
        out_shape=(
            jax.ShapeDtypeStruct((local_count, stride, hidden), BF16),
            jax.ShapeDtypeStruct((local_count, past, hidden), BF16),
        ),
        scratch_shapes=[
            pltpu.VMEM((stride, local_count, hidden), BF16),
            pltpu.VMEM((stride + past, channels, hidden), BF16),
            pltpu.SemaphoreType.DMA((stride + past,)),
        ],
        compiler_params=room(24),
        name="caches",
    )(near(arrived), near(tags), far(up_weight), up_bias)


def local(
    frames,
    row_dialogue,
    intersection_cache,
    history_cache,
    new_slot,
    up_weight,
    up_bias,
    dilated_weight,
    dilated_bias,
    project_weight,
    project_bias,
):
    local_count, frame_count, channels = frames.shape
    stride, hidden = intersection_cache.shape[1:]
    past = history_cache.shape[1]
    device_count = lax.axis_size("mp") * lax.axis_size("codec")
    capacity = 2 * local_count // device_count
    new_slot = new_slot[None]

    outgoing = bucket(row_dialogue[None], new_slot, frames, device_count, capacity)
    arrived = exchange(outgoing, device_count, capacity)
    prepared = (
        jnp.swapaxes(intersection_cache, 0, 1),
        jnp.swapaxes(history_cache, 0, 1),
        up_bias[None],
        dilated_bias[None],
        project_bias[None],
        select(new_slot, device_count * capacity, capacity),
    )
    arrived, prepared = lax.optimization_barrier((arrived, prepared))
    carried, history, up_bias, dilated_bias, project_bias, selector = prepared
    forwarded, tags = forward(arrived, selector, 2 * channels)
    arrived_caches = exchange(forwarded, device_count, capacity)
    upsampled = decode(
        arrived, carried, history, up_weight, up_bias, dilated_weight, dilated_bias, project_weight, project_bias
    )
    next_intersection, next_history = caches(arrived_caches, tags, up_weight, up_bias, local_count, stride, past)
    return (upsampled, next_intersection, next_history)


def solution(mesh):
    split = P(AXES)
    in_specs = (split,) * 5 + (P(),) * 6
    return jax.shard_map(local, mesh=mesh, in_specs=in_specs, out_specs=(split,) * 3, check_vma=False)
```
